32 devices in a mesh: slab: 8 (over y, x, core), angle: 4 (over z).
Axes of the slice: x: 2, y: 2, z: 4, core: 2. Of those that a mesh axis runs over, the one named last changes fastest.
Arguments:
- volume: float32 [2048, 1024], P('slab'), may hold values from 0.25 to 2
- system: bfloat16 [4, 1024, 2048], P('angle'), as said below
- measured: bfloat16 [4, 2048, 2048], P('angle', 'slab'), as said below
- band_weight: bfloat16 [4, 4, 2048], P(None, 'angle', 'slab'), may hold values from 0.25 to 1
- band_offset: int32 [4, 2048], P('angle', 'slab'), may hold values from 0 to 2044, as said below
- row_first: int32 [4, 8], P('angle'), may hold values from 0 to 1789, as said below
- row_count: int32 [4, 8], P('angle'), may hold values from 259 to 512, as said below
Outputs:
- updated: float32 [2048, 1024], P('slab')
The draws below stay inside these ranges and needn't reach their ends.
Inputs may be any that keep to these rules, and one draw needn't show every extreme that they name: `row_count`: every slab's window holds at most 512 rows; at every angle some slab's window holds exactly 512. row_first[a, s] = min(max(s * 256 + 256 // 2 - row_count[a, s] // 2, 0), 2048 - row_count[a, s]). `band_offset`: slice i of slab s starts its band at row_first[a, s] + (i (row_count[a, s] - 4)) // 255, so its 4 rows lie inside the slab's window. `system`: entries are nonnegative, and at every angle each pixel has positive entries. `measured`: entries are positive.
All inputs are finite; a program needn't handle non-finite values.
Results may differ from the reference program's by a relative error of at most 0.0003.
Values may be sent and summed in bfloat16 or wider, within the bound.
A program may use at most 64 MiB of HBM per device.

```python
import math
import jax
import jax.numpy as jnp
from jax import lax

SLICES = 256
PIXROWS = 8
PIXCOLS = 128
DET = 2048
BAND = 4
ANGLES = 4
DEPTH = 2048
PIXELS = 1024


def crossing_lists(key):
    nslab = DEPTH // SLICES
    key_count, key_busy = jax.random.split(jax.random.fold_in(key, 7))
    counts = jax.random.randint(key_count, (ANGLES, nslab), SLICES + BAND - 1, 2 * SLICES + 1)
    busiest = jax.random.randint(key_busy, (ANGLES,), 0, nslab)
    slab_ids = jnp.arange(nslab, dtype=jnp.int32)
    counts = jnp.where(slab_ids[None, :] == busiest[:, None], 2 * SLICES, counts).astype(jnp.int32)
    centres = slab_ids * SLICES + SLICES // 2
    starts = jnp.clip(centres[None, :] - counts // 2, 0, DEPTH - counts).astype(jnp.int32)
    inside = jnp.arange(SLICES, dtype=jnp.int32)
    offsets = starts[:, :, None] + inside[None, None, :] * (counts[:, :, None] - BAND) // (SLICES - 1)
    return (starts, counts, offsets.reshape(ANGLES, DEPTH).astype(jnp.int32))


def draw_row_first(key, part):
    return crossing_lists(key)[0]


def draw_row_count(key, part):
    return crossing_lists(key)[1]


def draw_band_offset(key, part):
    return crossing_lists(key)[2]


def draw_system(key, part):
    scale = DET // PIXCOLS
    key_slope, key_rough = jax.random.split(jax.random.fold_in(key, 11), 2)
    shape = (ANGLES, PIXROWS, PIXCOLS, DET)
    slopes = jax.random.uniform(key_slope, (ANGLES, 1, 1, 1), jnp.float32, -1.0, 1.0) * scale
    pix_rows = jnp.arange(PIXROWS, dtype=jnp.float32)[None, :, None, None]
    pix_cols = jnp.arange(PIXCOLS, dtype=jnp.float32)[None, None, :, None]
    centre = jnp.clip(scale * (pix_cols + 0.5) + slopes * (pix_rows - 0.5 * (PIXROWS - 1)), 1.0 * scale, 1.0 * (DET - scale))
    columns = jnp.arange(DET, dtype=jnp.float32)[None, None, None, :] + 0.5
    reach = 1.5 * scale
    tent = jnp.maximum(1.0 - jnp.abs(columns - centre) / reach, 0.0)
    rough = jnp.exp(jax.random.uniform(key_rough, shape, jnp.float32, jnp.log(0.25), jnp.log(4.0)))
    values = tent * rough / (2.0 * PIXROWS)
    return values.reshape(ANGLES, PIXELS, DET).astype(jnp.bfloat16)


def draw_measured(key, part):
    nslab = DEPTH // SLICES
    array_rows = jnp.arange(DEPTH, dtype=jnp.int32)
    detector_rows = array_rows % SLICES * nslab + array_rows // SLICES
    ramp = jnp.exp(jnp.log(4.0) * detector_rows.astype(jnp.float32) / DEPTH)
    values = jnp.exp(jax.random.uniform(key, (ANGLES, DEPTH, DET), jnp.float32, jnp.log(0.5), jnp.log(2.0)))
    return (values * ramp[None, :, None]).astype(jnp.bfloat16)


def steps_of(stream_key, dims, shards, low, high):
    gain, own = 1.0, jax.random.fold_in(stream_key, 6)
    for position, parts in shards:
        steps = jnp.exp(jax.random.uniform(jax.random.fold_in(own, position), (parts,), jnp.float32, low / len(shards), high / len(shards)))
        gain = gain * jnp.repeat(steps, dims[position] // parts).reshape([-1 if axis == position else 1 for axis in range(len(dims))])
    return gain


def setup_inputs(seed: int = 0) -> dict:
    keys = jax.random.split(jax.random.key(seed), 8)
    return {
        "volume": jnp.clip(jnp.exp(math.log(2.0) - 2.0794415 * jax.random.uniform(keys[0], (DEPTH, PIXELS), jnp.float32) ** steps_of(keys[0], (DEPTH, PIXELS), ((0, 8),), -0.2, 0.2)), 0.25, 2.0),
        "system": draw_system(jax.random.fold_in(keys[7], 71), 0),
        "measured": draw_measured(jax.random.fold_in(keys[7], 71), 0),
        "band_weight": jnp.clip(jnp.exp(math.log(1.0) - 1.3862944 * jax.random.uniform(keys[3], (BAND, ANGLES, DEPTH), jnp.float32) ** steps_of(keys[3], (BAND, ANGLES, DEPTH), ((1, 4), (2, 8)), -0.2, 0.2)), 0.25, 1.0).astype(jnp.bfloat16),
        "band_offset": draw_band_offset(jax.random.fold_in(keys[7], 71), 0),
        "row_first": draw_row_first(jax.random.fold_in(keys[7], 71), 0),
        "row_count": draw_row_count(jax.random.fold_in(keys[7], 71), 0),
    }


SMOOTHING = 0.5
TV_STEP = 0.2
FLOOR = 0.5

def smooth_slope(differ):
    return differ / jnp.sqrt(differ * differ + SMOOTHING * SMOOTHING)

def band_matrix(weights, offsets, starts, counts, width):
    columns = jnp.arange(width, dtype=jnp.int32)
    relative = (offsets - starts[..., None])[..., None]
    matrix = jnp.zeros(relative.shape[:-1] + (width,), jnp.float32)
    for band_row in range(weights.shape[0]):
        matrix = matrix + weights[band_row][..., None].astype(jnp.float32) * (relative + band_row == columns).astype(jnp.float32)
    return matrix * (columns < counts[..., None, None]).astype(jnp.float32)

def tv_gradient(field):
    gradient = jnp.zeros(field.shape, jnp.float32)
    for axis_id in range(3):
        slopes = smooth_slope(jnp.diff(field, axis=axis_id))
        before = [(0, 0), (0, 0), (0, 0)]
        after = [(0, 0), (0, 0), (0, 0)]
        before[axis_id] = (1, 0)
        after[axis_id] = (0, 1)
        gradient = gradient + jnp.pad(slopes, before) - jnp.pad(slopes, after)
    return gradient

def reference(volume, system, measured, band_weight, band_offset, row_first, row_count):
    nslab = DEPTH // SLICES
    width = 2 * SLICES
    volume_b = volume.astype(jnp.bfloat16)
    weights_by_angle = jnp.transpose(band_weight, (1, 0, 2))

    def one_angle(carry, inputs):
        back_sum, weight_sum = carry
        matrix_a, measured_a, weights_a, offsets_a, starts_a, counts_a = inputs
        line_b = jnp.dot(volume_b, matrix_a, preferred_element_type=jnp.float32).astype(jnp.bfloat16)
        line_b = lax.optimization_barrier(line_b)
        line = line_b.astype(jnp.float32)
        bands = band_matrix(weights_a.reshape(BAND, nslab, SLICES), offsets_a.reshape(nslab, SLICES), starts_a, counts_a, width)
        contrib = jnp.einsum('sic,siu->scu', bands, line.reshape(nslab, SLICES, DET), precision=lax.Precision.HIGHEST)
        weight_rows = lax.optimization_barrier(jnp.sum(bands, axis=1))
        rows = starts_a[:, None] + jnp.arange(width, dtype=jnp.int32)[None, :]
        forward = jnp.zeros((DEPTH, DET), jnp.float32).at[rows.reshape(-1)].add(contrib.reshape(-1, DET), mode='drop')
        row_weight = jnp.zeros((DEPTH,), jnp.float32).at[rows.reshape(-1)].add(weight_rows.reshape(-1), mode='drop')
        measured_rows = measured_a.reshape(nslab, SLICES, DET).transpose(1, 0, 2).reshape(DEPTH, DET)
        column_sums = lax.optimization_barrier(jnp.sum(matrix_a.astype(jnp.float32), axis=0))
        pixel_sums = lax.optimization_barrier(jnp.sum(matrix_a.astype(jnp.float32), axis=1))
        scaled = ((measured_rows.astype(jnp.float32) - forward) / jnp.maximum(row_weight[:, None] * column_sums[None, :], FLOOR)).astype(jnp.bfloat16)
        valid = rows < DEPTH
        gathered = jnp.where(valid[..., None], scaled[jnp.minimum(rows, DEPTH - 1)].astype(jnp.float32), jnp.float32(0.0))
        spread = jnp.einsum('sic,scu->siu', bands, gathered, precision=lax.Precision.HIGHEST).astype(jnp.bfloat16).reshape(DEPTH, DET)
        back = jnp.dot(spread, matrix_a.T, preferred_element_type=jnp.float32)
        weight_cols = lax.optimization_barrier(jnp.sum(weights_a.astype(jnp.float32), axis=0))[:, None] * pixel_sums[None, :]
        return ((back_sum + back, weight_sum + weight_cols), None)
    start_state = (jnp.zeros((DEPTH, PIXELS), jnp.float32), jnp.zeros((DEPTH, PIXELS), jnp.float32))
    (back_sum, weight_sum), _ = lax.scan(one_angle, start_state, (system, measured, weights_by_angle, band_offset, row_first, row_count))
    middle = volume + back_sum / weight_sum
    gradient = tv_gradient(middle.reshape(DEPTH, PIXROWS, PIXCOLS)).reshape(DEPTH, PIXELS)
    return middle - TV_STEP * gradient
```

```python
import functools

import jax
import jax.numpy as jnp
from jax import lax
from jax.experimental import pallas as pl
from jax.experimental.pallas import tpu as pltpu
from jax.sharding import PartitionSpec as P

SMOOTHING = 0.5
TV_STEP = 0.2
FLOOR = 0.5
TILE = 512
FAR = 128
LANES = 128


def smooth_slope(differ):
    return differ * lax.rsqrt(differ * differ + SMOOTHING * SMOOTHING)


def kernel(
    n, m, vol_ref, small_ref, sys_ref, meas_ref, out_ref,
    sysv, volx, smallx, win, fwd, inv, spread, band_t, band_own, col_sum, pack, packs,
    acc, recv_a, recv_b, total, mid, edge_lo, edge_hi, halo_prev, halo_next,
    sys_sem, own_sem, vol_send, vol_recv, small_send, small_recv, win_send, win_recv,
    pack_send, pack_recv, a_send, a_recv, b_send, b_recv, edge_send, edge_recv,
):
    me = lax.axis_index("slab")
    ang = lax.axis_index("angle")
    slices, pixels = vol_ref.shape
    detector = sysv.shape[1]
    width = 2 * slices
    chunks = pixels // LANES
    half = m // 2
    f32, bf16 = jnp.float32, jnp.bfloat16

    def slab_peer(k):
        return lax.rem(me + k, n)

    def angle_peer(k):
        return lax.rem(ang + k, m)

    def first_block(slab):
        return jnp.clip(2 * slab - 1, 0, 2 * n - 4)

    def remote(src, dst, send, recv, axis, peer):
        return pltpu.make_async_remote_copy(
            src_ref=src, dst_ref=dst, send_sem=send, recv_sem=recv,
            device_id={axis: peer}, device_id_type=pl.DeviceIdType.MESH,
        )

    barrier = pltpu.get_barrier_semaphore()
    for k in range(1, n):
        pl.semaphore_signal(barrier, inc=1, device_id={"slab": slab_peer(k)},
                            device_id_type=pl.DeviceIdType.MESH)
    for k in range(1, m):
        pl.semaphore_signal(barrier, inc=1, device_id={"angle": angle_peer(k)},
                            device_id_type=pl.DeviceIdType.MESH)
    sys_copy = pltpu.make_async_copy(sys_ref, sysv, sys_sem)
    sys_copy.start()
    own_copy = pltpu.make_async_copy(meas_ref.at[pl.ds(first_block(me), 4)], win.at[me], own_sem)
    own_copy.start()
    own = pl.ds(0, slices)
    volx[own, :] = vol_ref[...].astype(bf16)
    smallx[:, own] = small_ref[...]
    has_prev, has_next = me > 0, me < n - 1
    prev_at, next_at, far_at = slices, 2 * slices, 3 * slices
    far_up = jnp.logical_or(me == 0, me == n - 3)
    far_down = jnp.logical_or(me == 2, me == n - 1)
    has_far = jnp.logical_or(far_up, far_down)

    def clear(start, size):
        volx[pl.ds(start, size), :] = jnp.zeros((size, pixels), bf16)
        smallx[:, pl.ds(start, size)] = jnp.zeros((8, size), f32)

    @pl.when(jnp.logical_not(has_prev))
    def _():
        clear(prev_at, slices)

    @pl.when(jnp.logical_not(has_next))
    def _():
        clear(next_at, slices)

    @pl.when(jnp.logical_not(has_far))
    def _():
        clear(far_at, FAR)

    pl.semaphore_wait(barrier, n + m - 2)

    def halo(slot, src_at, dst_at, size, peer):
        return (
            remote(smallx.at[:, pl.ds(src_at, size)], smallx.at[:, pl.ds(dst_at, size)],
                   small_send.at[slot], small_recv.at[slot], "slab", peer),
            remote(volx.at[pl.ds(src_at, size)], volx.at[pl.ds(dst_at, size)],
                   vol_send.at[slot], vol_recv.at[slot], "slab", peer),
        )

    to_next = halo(0, 0, prev_at, slices, lax.rem(me + 1, n))
    to_prev = halo(1, 0, next_at, slices, lax.rem(me + n - 1, n))
    to_up = halo(2, slices - FAR, far_at, FAR, lax.rem(me + 2, n))
    to_down = halo(2, 0, far_at, FAR, lax.rem(me + n - 2, n))
    moves = ((has_next, to_next), (has_prev, to_prev), (far_up, to_up), (far_down, to_down))
    arrivals = ((has_prev, to_next), (has_next, to_prev), (has_far, to_up))
    for condition, copies in moves:
        @pl.when(condition)
        def _():
            for copy in copies:
                copy.start()

    shares = []
    for k in range(1, n):
        peer = slab_peer(k)
        shares.append(remote(meas_ref.at[pl.ds(first_block(peer), 4)], win.at[me],
                             win_send.at[k], win_recv.at[k], "slab", peer))
    for copy in shares:
        copy.start()

    sys_copy.wait()
    col_sum[...] = jnp.dot(jnp.ones((8, pixels), bf16), sysv[...], preferred_element_type=f32)
    pixel_sum = lax.dot_general(jnp.ones((8, detector), bf16), sysv[...],
                                (((1,), (1,)), ((), ())), preferred_element_type=f32)
    keep = lax.broadcasted_iota(jnp.int32, (8, 1), 0) == 0
    pack[:, pl.ds(0, pixels)] = jnp.where(keep, pixel_sum, 0.0)
    weight_total = jnp.sum(small_ref[0:4, :], axis=0, keepdims=True)
    pack[:, pl.ds(pixels, slices)] = jnp.where(keep, weight_total, 0.0)
    packs[pl.ds(ang, 1)] = pack[...][None]
    pack_copies = [
        remote(pack, packs.at[ang], pack_send.at[k], pack_recv.at[k], "angle", angle_peer(k))
        for k in range(1, m)
    ]
    for copy in pack_copies:
        copy.start()

    for condition, copies in arrivals:
        @pl.when(condition)
        def _():
            for copy in copies:
                copy.wait_recv()

    share = width // n
    position = lax.broadcasted_iota(jnp.int32, (width, 1), 0)
    source = lax.shift_right_logical(position, share.bit_length() - 1)
    row = first_block(me) * (slices // 2) + lax.bitwise_and(position, share - 1) * n + source
    row = row.astype(f32)
    row_weight = jnp.zeros((width, 1), f32)
    for start in range(0, volx.shape[0], FAR):
        at = pl.ds(start, FAR)
        behind = row - smallx[4:5, at]
        block = jnp.zeros((width, FAR), f32)
        for k in range(4):
            block = jnp.where(behind == float(k), smallx[k : k + 1, at], block)
        row_weight = row_weight + jnp.sum(block, axis=1, keepdims=True)
        band_t[:, at] = block.astype(bf16)
        if start < slices:
            band_own[at, :] = block.T.astype(bf16)

    @pl.loop(0, detector // TILE)
    def _(step):
        at = pl.ds(pl.multiple_of(step * TILE, TILE), TILE)
        line = jnp.dot(volx[...], sysv[:, at], preferred_element_type=f32).astype(bf16)
        fwd[:, at] = jnp.dot(band_t[...], line, preferred_element_type=f32)
        inv[:, at] = 1.0 / jnp.maximum(row_weight * col_sum[0:1, at], FLOOR)

    own_copy.wait()
    for copy in shares:
        copy.wait_recv()

    @pl.loop(0, detector // TILE)
    def _(step):
        at = pl.ds(pl.multiple_of(step * TILE, TILE), TILE)
        rows = win[:, :, :, at].astype(f32).reshape(width, TILE)
        residual = ((rows - fwd[:, at]) * inv[:, at]).astype(bf16)
        spread[:, at] = jnp.dot(band_own[...], residual, preferred_element_type=f32).astype(bf16)

    for copy in pack_copies:
        copy.wait_recv()

    left = ang < half
    inner = jnp.where(left, ang + 1, ang - 1)
    outer = jnp.where(left, jnp.maximum(ang - 1, 0), jnp.minimum(ang + 1, m - 1))
    centre = jnp.logical_or(ang == half - 1, ang == half)
    has_outer = jnp.logical_and(ang > 0, ang < m - 1)
    not_centre = jnp.logical_not(centre)
    no_outer = jnp.logical_not(has_outer)

    def up_copy(c, target):
        sem = a_recv if target is recv_a else b_recv
        return remote(acc.at[c], target.at[c], a_send.at[c], sem.at[c], "angle", inner)

    def down_copy(c):
        return remote(total.at[c], recv_b.at[c], b_send.at[c], b_recv.at[c], "angle", outer)

    def multiply(pair):
        product = lax.dot_general(spread[...], sysv[pl.ds(pair * 2 * LANES, 2 * LANES), :],
                                  (((1,), (1,)), ((), ())), preferred_element_type=f32)
        acc[2 * pair] = product[:, :LANES]
        acc[2 * pair + 1] = product[:, LANES:]

    def collect(c):
        @pl.when(has_outer)
        def _():
            up_copy(c, recv_a).wait_recv()
            acc[c] = acc[c] + recv_a[c]

        @pl.when(centre)
        def _():
            up_copy(c, recv_b).start()

        @pl.when(not_centre)
        def _():
            up_copy(c, recv_a).start()

    all_packs = packs[...].reshape(m * 8, pixels + slices)

    def finish(c):
        down_copy(c).wait_recv()
        at = pl.ds(c * LANES, LANES)
        whole = jnp.where(centre, acc[c] + recv_b[c], recv_b[c])
        total[c] = whole

        @pl.when(has_outer)
        def _():
            down_copy(c).start()

        weight = lax.dot_general(
            all_packs[:, pixels:], all_packs[:, c * LANES : (c + 1) * LANES],
            (((0,), (0,)), ((), ())), precision=lax.Precision.HIGHEST, preferred_element_type=f32,
        )
        cells = vol_ref[:, at] + whole / weight
        mid[c] = cells
        edge_lo[c : c + 1, :] = cells[0:1, :]
        edge_hi[c : c + 1, :] = cells[slices - 1 : slices, :]

    def run(lag):
        for c in range(chunks + lag):
            if c < chunks:
                if c % 2 == 0:
                    multiply(c // 2)
                collect(c)
            if c >= lag:
                finish(c - lag)

    @pl.when(has_outer)
    def _():
        run(2)

    @pl.when(no_outer)
    def _():
        run(chunks)

    edge_up = remote(edge_hi, halo_prev, edge_send.at[0], edge_recv.at[0], "slab", lax.rem(me + 1, n))
    edge_down = remote(edge_lo, halo_next, edge_send.at[1], edge_recv.at[1], "slab", lax.rem(me + n - 1, n))

    @pl.when(has_next)
    def _():
        edge_up.start()

    @pl.when(has_prev)
    def _():
        edge_down.start()

    @pl.when(jnp.logical_not(has_prev))
    def _():
        halo_prev[...] = edge_lo[...]

    @pl.when(jnp.logical_not(has_next))
    def _():
        halo_next[...] = edge_hi[...]

    lane = lax.broadcasted_iota(jnp.int32, (1, LANES), 1)
    below = None
    for c in range(chunks):
        cells = mid[c]
        slope = jnp.where(lane < LANES - 1,
                          smooth_slope(pltpu.roll(cells, LANES - 1, axis=1) - cells), 0.0)
        gradient = pltpu.roll(slope, 1, axis=1) - slope
        if below is not None:
            gradient = gradient + below
        if c + 1 < chunks:
            below = smooth_slope(mid[c + 1] - cells)
            gradient = gradient - below
        total_at = pl.ds(c * LANES, LANES)
        out_ref[:, total_at] = gradient

    @pl.when(has_prev)
    def _():
        edge_up.wait_recv()

    @pl.when(has_next)
    def _():
        edge_down.wait_recv()

    for c in range(chunks):
        at = pl.ds(c * LANES, LANES)
        cells = mid[c]
        upper = jnp.concatenate([cells[1:, :], halo_next[c : c + 1, :]], axis=0)
        slope = smooth_slope(upper - cells)
        first = smooth_slope(cells[0:1, :] - halo_prev[c : c + 1, :])
        lower = jnp.concatenate([first, slope[: slices - 1, :]], axis=0)
        out_ref[:, at] = cells - TV_STEP * (out_ref[:, at] + lower - slope)

    for condition, copies in moves:
        @pl.when(condition)
        def _():
            for copy in copies:
                copy.wait_send()
    for copy in shares + pack_copies:
        copy.wait_send()
    for c in range(chunks):
        up_copy(c, recv_a).wait_send()

        @pl.when(has_outer)
        def _():
            down_copy(c).wait_send()

    @pl.when(has_next)
    def _():
        edge_up.wait_send()

    @pl.when(has_prev)
    def _():
        edge_down.wait_send()


def body(n, m, volume, system, measured, band_weight, band_offset, row_first, row_count):
    slices, pixels = volume.shape
    detector = system.shape[2]
    grain = slices // 2 // n
    width = 2 * slices
    chunks = pixels // LANES
    extended = 3 * slices + FAR
    small = jnp.concatenate(
        [
            band_weight[:, 0, :].astype(jnp.float32),
            band_offset.astype(jnp.float32),
            jnp.zeros((3, slices), jnp.float32),
        ],
        axis=0,
    )
    f32, bf16 = jnp.float32, jnp.bfloat16
    dma = pltpu.SemaphoreType.DMA
    chunk = pltpu.VMEM((chunks, slices, LANES), f32)
    edge = pltpu.VMEM((chunks, LANES), f32)
    vmem = pl.BlockSpec(memory_space=pltpu.VMEM)
    return pl.pallas_call(
        functools.partial(kernel, n, m),
        out_shape=jax.ShapeDtypeStruct((slices, pixels), f32),
        in_specs=[vmem, vmem, pl.BlockSpec(memory_space=pl.ANY), pl.BlockSpec(memory_space=pl.ANY)],
        out_specs=vmem,
        scratch_shapes=[
            pltpu.VMEM((pixels, detector), bf16),
            pltpu.VMEM((extended, pixels), bf16),
            pltpu.VMEM((8, extended), f32),
            pltpu.VMEM((n, 4, grain, detector), bf16),
            pltpu.VMEM((width, detector), f32),
            pltpu.VMEM((width, detector), f32),
            pltpu.VMEM((slices, detector), bf16),
            pltpu.VMEM((width, extended), bf16),
            pltpu.VMEM((slices, width), bf16),
            pltpu.VMEM((8, detector), f32),
            pltpu.VMEM((8, pixels + slices), f32),
            pltpu.VMEM((m, 8, pixels + slices), f32),
            chunk, chunk, chunk, chunk, chunk,
            edge, edge, edge, edge,
            dma, dma,
            dma((3,)), dma((3,)), dma((3,)), dma((3,)), dma((n,)), dma((n,)),
            dma((m,)), dma((m,)),
            dma((chunks,)), dma((chunks,)), dma((chunks,)), dma((chunks,)),
            dma((2,)), dma((2,)),
        ],
        compiler_params=pltpu.CompilerParams(
            collective_id=0, has_side_effects=True, vmem_limit_bytes=56 * 1024 * 1024
        ),
    )(volume, small, system[0], measured[0].reshape(2 * n, grain, detector))


def solution(mesh):
    return jax.shard_map(
        functools.partial(body, mesh.shape["slab"], mesh.shape["angle"]),
        mesh=mesh,
        in_specs=(
            P("slab", None),
            P("angle", None, None),
            P("angle", "slab", None),
            P(None, "angle", "slab"),
            P("angle", "slab"),
            P("angle", None),
            P("angle", None),
        ),
        out_specs=P("slab", None),
        check_vma=False,
    )
```

```python
import functools

import jax
import jax.numpy as jnp
from jax import lax
from jax.experimental import pallas as pl
from jax.experimental.pallas import tpu as pltpu
from jax.sharding import PartitionSpec as P

SMOOTHING = 0.5
TV_STEP = 0.2
FLOOR = 0.5
TILE = 512
FAR = 128
NEAR_ROWS = 144
FAR_ROWS = 80
PARTS = 2
LANES = 128


def smooth_slope(differ):
    return differ * lax.rsqrt(differ * differ + SMOOTHING * SMOOTHING)


def kernel(
    n, m, vol_ref, small_ref, sys_ref, meas_ref, out_ref,
    sysv, volx, smallx, win, fwd, inv, spread, band_t, band_own, col_sum, pack, packs,
    acc, recv_a, recv_b, total, mid, edge_lo, edge_hi, halo_prev, halo_next,
    sys_sem, own_sem, vol_send, vol_recv, small_send, small_recv, win_send, win_recv,
    relay_send, relay_recv, pack_send, pack_recv, a_send, a_recv, b_send, b_recv, edge_send, edge_recv,
):
    me = lax.axis_index("slab")
    ang = lax.axis_index("angle")
    slices, pixels = vol_ref.shape
    detector = sysv.shape[1]
    width = 2 * slices
    chunks = pixels // LANES
    piece = slices // PARTS
    half = m // 2
    chip, core = me // 2, lax.rem(me, 2)
    partner = chip * 2 + 1 - core
    f32, bf16 = jnp.float32, jnp.bfloat16

    def slab_peer(k):
        return lax.rem(me + k, n)

    def angle_peer(k):
        return lax.rem(ang + k, m)

    def first_block(slab):
        return jnp.clip(2 * slab - 1, 0, 2 * n - 4)

    def remote(src, dst, send, recv, axis, peer):
        return pltpu.make_async_remote_copy(
            src_ref=src, dst_ref=dst, send_sem=send, recv_sem=recv,
            device_id={axis: peer}, device_id_type=pl.DeviceIdType.MESH,
        )

    extra = volx.shape[0] - slices
    volx[pl.ds(slices, extra), :] = jnp.zeros((extra, pixels), bf16)
    smallx[:, pl.ds(slices, extra)] = jnp.zeros((8, extra), f32)
    barrier = pltpu.get_barrier_semaphore()
    for k in range(1, n):
        pl.semaphore_signal(barrier, inc=1, device_id={"slab": slab_peer(k)},
                            device_id_type=pl.DeviceIdType.MESH)
    for k in range(1, m):
        pl.semaphore_signal(barrier, inc=1, device_id={"angle": angle_peer(k)},
                            device_id_type=pl.DeviceIdType.MESH)
    sys_copy = pltpu.make_async_copy(sys_ref, sysv, sys_sem)
    sys_copy.start()
    own_copy = pltpu.make_async_copy(meas_ref.at[pl.ds(first_block(me), 4)], win.at[me], own_sem)
    own_copy.start()
    own = pl.ds(0, slices)
    volx[own, :] = vol_ref[...].astype(bf16)
    smallx[:, own] = small_ref[...]
    has_prev, has_next = me > 0, me < n - 1
    prev_at, next_at, far_at = slices, 2 * slices, 3 * slices
    far_up = jnp.logical_or(me == 0, me == n - 3)
    far_down = jnp.logical_or(me == 2, me == n - 1)
    has_far = jnp.logical_or(far_up, far_down)

    pl.semaphore_wait(barrier, n + m - 2)

    def halo(slot, src_at, dst_at, size, src_row, dst_row, rows, peer):
        return (
            remote(smallx.at[:, pl.ds(src_at, size)], smallx.at[:, pl.ds(dst_at, size)],
                   small_send.at[slot], small_recv.at[slot], "slab", peer),
            remote(volx.at[pl.ds(src_row, rows)], volx.at[pl.ds(dst_row, rows)],
                   vol_send.at[slot], vol_recv.at[slot], "slab", peer),
        )

    above, under = lax.rem(me + 1, n), lax.rem(me + n - 1, n)
    cut = slices - NEAR_ROWS
    next_all = halo(0, 0, prev_at, slices, 0, prev_at, slices, above)
    next_part = halo(0, 0, prev_at, slices, cut, prev_at + cut, NEAR_ROWS, above)
    prev_all = halo(1, 0, next_at, slices, 0, next_at, slices, under)
    prev_part = halo(1, 0, next_at, slices, 0, next_at, NEAR_ROWS, under)
    far_cut = FAR - FAR_ROWS
    to_up = halo(2, slices - FAR, far_at, FAR, slices - FAR_ROWS, far_at + far_cut, FAR_ROWS,
                 lax.rem(me + 2, n))
    to_down = halo(2, 0, far_at, FAR, 0, far_at, FAR_ROWS, lax.rem(me + n - 2, n))
    both, either, no = jnp.logical_and, jnp.logical_or, jnp.logical_not
    send_up_all = either(me == 0, me == n - 2)
    send_down_all = either(me == n - 1, me == 1)
    get_prev_all = either(me == 1, me == n - 1)
    get_next_all = either(me == n - 2, me == 0)
    moves = (
        (both(has_next, send_up_all), next_all),
        (both(has_next, no(send_up_all)), next_part),
        (both(has_prev, send_down_all), prev_all),
        (both(has_prev, no(send_down_all)), prev_part),
        (far_up, to_up),
        (far_down, to_down),
    )
    arrivals = (
        (both(has_prev, get_prev_all), next_all),
        (both(has_prev, no(get_prev_all)), next_part),
        (both(has_next, get_next_all), prev_all),
        (both(has_next, no(get_next_all)), prev_part),
        (far_down, to_up),
        (far_up, to_down),
    )
    for condition, copies in moves:
        @pl.when(condition)
        def _():
            for copy in copies:
                copy.start()

    chips = n // 2
    shares, gets, relays, relay_gets = [], [], [], []
    shift = first_block(chip * 2 + 1) - first_block(chip * 2)
    relay_from = jnp.where(core == 0, shift, 3 - shift)
    for d in range(1, chips):
        for e in range(2):
            slot = 2 * d + e
            peer = lax.rem(chip + d, chips) * 2 + e
            shares.append(remote(
                meas_ref.at[pl.ds(first_block(peer) + e, 3)], win.at[me, pl.ds(e, 3)],
                win_send.at[slot], win_recv.at[2 * d + core], "slab", peer))
            source = lax.rem(chip + chips - d, chips) * 2 + e
            gets.append(remote(
                meas_ref.at[pl.ds(0, 3)], win.at[source, pl.ds(core, 3)],
                win_send.at[slot], win_recv.at[slot], "slab", peer))
            relays.append(remote(
                win.at[source, pl.ds(relay_from, 1)], win.at[source, pl.ds(3 * core, 1)],
                relay_send.at[slot], relay_recv.at[slot], "slab", partner))
            relay_gets.append(remote(
                win.at[source, pl.ds(relay_from, 1)], win.at[source, pl.ds(3 - 3 * core, 1)],
                relay_send.at[slot], relay_recv.at[slot], "slab", partner))
    beside = remote(meas_ref.at[pl.ds(first_block(partner), 4)], win.at[me],
                    win_send.at[0], win_recv.at[0], "slab", partner)
    beside_get = remote(meas_ref.at[pl.ds(0, 4)], win.at[partner],
                        win_send.at[0], win_recv.at[0], "slab", partner)
    for copy in shares + [beside]:
        copy.start()

    sys_copy.wait()
    col_sum[...] = jnp.dot(jnp.ones((8, pixels), bf16), sysv[...], preferred_element_type=f32)
    pixel_sum = lax.dot_general(jnp.ones((8, detector), bf16), sysv[...],
                                (((1,), (1,)), ((), ())), preferred_element_type=f32)
    keep = lax.broadcasted_iota(jnp.int32, (8, 1), 0) == 0
    pack[:, pl.ds(0, pixels)] = jnp.where(keep, pixel_sum, 0.0)
    weight_total = jnp.sum(small_ref[0:4, :], axis=0, keepdims=True)
    pack[:, pl.ds(pixels, slices)] = jnp.where(keep, weight_total, 0.0)
    packs[pl.ds(ang, 1)] = pack[...][None]
    pack_copies = [
        remote(pack, packs.at[ang], pack_send.at[k], pack_recv.at[k], "angle", angle_peer(k))
        for k in range(1, m)
    ]
    for copy in pack_copies:
        copy.start()

    for condition, copies in arrivals:
        @pl.when(condition)
        def _():
            for copy in copies:
                copy.wait_recv()

    share = width // n
    position = lax.broadcasted_iota(jnp.int32, (width, 1), 0)
    source = lax.shift_right_logical(position, share.bit_length() - 1)
    row = first_block(me) * (slices // 2) + lax.bitwise_and(position, share - 1) * n + source
    row = row.astype(f32)
    row_weight = jnp.zeros((width, 1), f32)
    for start in range(0, volx.shape[0], FAR):
        at = pl.ds(start, FAR)
        behind = row - smallx[4:5, at]
        block = jnp.zeros((width, FAR), f32)
        for k in range(4):
            block = jnp.where(behind == float(k), smallx[k : k + 1, at], block)
        row_weight = row_weight + jnp.sum(block, axis=1, keepdims=True)
        band_t[:, at] = block.astype(bf16)
        if start < slices:
            band_own[at, :] = block.T.astype(bf16)

    @pl.loop(0, detector // TILE)
    def _(step):
        at = pl.ds(pl.multiple_of(step * TILE, TILE), TILE)
        line = jnp.dot(volx[...], sysv[:, at], preferred_element_type=f32).astype(bf16)
        fwd[:, at] = jnp.dot(band_t[...], line, preferred_element_type=f32)
        inv[:, at] = 1.0 / jnp.maximum(row_weight * col_sum[0:1, at], FLOOR)

    own_copy.wait()
    for get, relay in zip(gets, relays):
        get.wait_recv()
        relay.start()
    beside_get.wait_recv()
    for get in relay_gets:
        get.wait_recv()

    @pl.loop(0, detector // TILE)
    def _(step):
        at = pl.ds(pl.multiple_of(step * TILE, TILE), TILE)
        rows = win[:, :, :, at].astype(f32).reshape(width, TILE)
        residual = ((rows - fwd[:, at]) * inv[:, at]).astype(bf16)
        spread[:, at] = jnp.dot(band_own[...], residual, preferred_element_type=f32).astype(bf16)

    for copy in pack_copies:
        copy.wait_recv()

    left = ang < half
    inner = jnp.where(left, ang + 1, ang - 1)
    outer = jnp.where(left, jnp.maximum(ang - 1, 0), jnp.minimum(ang + 1, m - 1))
    centre = jnp.logical_or(ang == half - 1, ang == half)
    has_outer = jnp.logical_and(ang > 0, ang < m - 1)
    not_centre = jnp.logical_not(centre)
    no_outer = jnp.logical_not(has_outer)

    def up_copy(c, target):
        sem = a_recv if target is recv_a else b_recv
        return remote(acc.at[c], target.at[c], a_send.at[c], sem.at[c], "angle", inner)

    def down_copy(c):
        return remote(total.at[c], recv_b.at[c], b_send.at[c], b_recv.at[c], "angle", outer)

    def multiply(pair):
        product = lax.dot_general(spread[...], sysv[pl.ds(pair * 2 * LANES, 2 * LANES), :],
                                  (((1,), (1,)), ((), ())), preferred_element_type=f32)
        for c in range(2):
            for part in range(PARTS):
                acc[(2 * pair + c) * PARTS + part] = product[
                    part * piece : (part + 1) * piece, c * LANES : (c + 1) * LANES
                ]

    def collect(c):
        @pl.when(has_outer)
        def _():
            up_copy(c, recv_a).wait_recv()
            acc[c] = acc[c] + recv_a[c]

        @pl.when(centre)
        def _():
            up_copy(c, recv_b).start()

        @pl.when(not_centre)
        def _():
            up_copy(c, recv_a).start()

    all_packs = packs[...].reshape(m * 8, pixels + slices)

    def finish(index):
        down_copy(index).wait_recv()
        c, part = index // PARTS, index % PARTS
        first = part * piece
        whole = jnp.where(centre, acc[index] + recv_b[index], recv_b[index])
        total[index] = whole

        @pl.when(has_outer)
        def _():
            down_copy(index).start()

        weight = lax.dot_general(
            all_packs[:, pixels + first : pixels + first + piece],
            all_packs[:, c * LANES : (c + 1) * LANES],
            (((0,), (0,)), ((), ())), precision=lax.Precision.HIGHEST, preferred_element_type=f32,
        )
        rows = pl.ds(first, piece)
        cells = vol_ref[rows, pl.ds(c * LANES, LANES)] + whole / weight
        mid[c, rows] = cells
        if part == 0:
            edge_lo[c : c + 1, :] = cells[0:1, :]
        if part == PARTS - 1:
            edge_hi[c : c + 1, :] = cells[piece - 1 : piece, :]

    pieces = chunks * PARTS

    def run(lag):
        for index in range(pieces + lag):
            if index < pieces:
                if index % (2 * PARTS) == 0:
                    multiply(index // (2 * PARTS))
                collect(index)
            if index >= lag:
                finish(index - lag)

    @pl.when(has_outer)
    def _():
        run(2)

    @pl.when(no_outer)
    def _():
        run(pieces)

    edge_up = remote(edge_hi, halo_prev, edge_send.at[0], edge_recv.at[0], "slab", lax.rem(me + 1, n))
    edge_down = remote(edge_lo, halo_next, edge_send.at[1], edge_recv.at[1], "slab", lax.rem(me + n - 1, n))

    @pl.when(has_next)
    def _():
        edge_up.start()

    @pl.when(has_prev)
    def _():
        edge_down.start()

    @pl.when(jnp.logical_not(has_prev))
    def _():
        halo_prev[...] = edge_lo[...]

    @pl.when(jnp.logical_not(has_next))
    def _():
        halo_next[...] = edge_hi[...]

    lane = lax.broadcasted_iota(jnp.int32, (1, LANES), 1)
    below = None
    for c in range(chunks):
        cells = mid[c]
        slope = jnp.where(lane < LANES - 1,
                          smooth_slope(pltpu.roll(cells, LANES - 1, axis=1) - cells), 0.0)
        gradient = pltpu.roll(slope, 1, axis=1) - slope
        if below is not None:
            gradient = gradient + below
        if c + 1 < chunks:
            below = smooth_slope(mid[c + 1] - cells)
            gradient = gradient - below
        total_at = pl.ds(c * LANES, LANES)
        out_ref[:, total_at] = gradient

    @pl.when(has_prev)
    def _():
        edge_up.wait_recv()

    @pl.when(has_next)
    def _():
        edge_down.wait_recv()

    for c in range(chunks):
        at = pl.ds(c * LANES, LANES)
        cells = mid[c]
        upper = jnp.concatenate([cells[1:, :], halo_next[c : c + 1, :]], axis=0)
        slope = smooth_slope(upper - cells)
        first = smooth_slope(cells[0:1, :] - halo_prev[c : c + 1, :])
        lower = jnp.concatenate([first, slope[: slices - 1, :]], axis=0)
        out_ref[:, at] = cells - TV_STEP * (out_ref[:, at] + lower - slope)

    for condition, copies in moves:
        @pl.when(condition)
        def _():
            for copy in copies:
                copy.wait_send()
    for copy in shares + [beside] + relays + pack_copies:
        copy.wait_send()
    for c in range(pieces):
        up_copy(c, recv_a).wait_send()

        @pl.when(has_outer)
        def _():
            down_copy(c).wait_send()

    @pl.when(has_next)
    def _():
        edge_up.wait_send()

    @pl.when(has_prev)
    def _():
        edge_down.wait_send()


def body(n, m, volume, system, measured, band_weight, band_offset, row_first, row_count):
    slices, pixels = volume.shape
    detector = system.shape[2]
    grain = slices // 2 // n
    width = 2 * slices
    chunks = pixels // LANES
    extended = 3 * slices + FAR
    small = jnp.concatenate(
        [
            band_weight[:, 0, :].astype(jnp.float32),
            band_offset.astype(jnp.float32),
            jnp.zeros((3, slices), jnp.float32),
        ],
        axis=0,
    )
    f32, bf16 = jnp.float32, jnp.bfloat16
    dma = pltpu.SemaphoreType.DMA
    chunk = pltpu.VMEM((chunks * PARTS, slices // PARTS, LANES), f32)
    edge = pltpu.VMEM((chunks, LANES), f32)
    vmem = pl.BlockSpec(memory_space=pltpu.VMEM)
    return pl.pallas_call(
        functools.partial(kernel, n, m),
        out_shape=jax.ShapeDtypeStruct((slices, pixels), f32),
        in_specs=[vmem, vmem, pl.BlockSpec(memory_space=pl.ANY), pl.BlockSpec(memory_space=pl.ANY)],
        out_specs=vmem,
        scratch_shapes=[
            pltpu.VMEM((pixels, detector), bf16),
            pltpu.VMEM((extended, pixels), bf16),
            pltpu.VMEM((8, extended), f32),
            pltpu.VMEM((n, 4, grain, detector), bf16),
            pltpu.VMEM((width, detector), f32),
            pltpu.VMEM((width, detector), f32),
            pltpu.VMEM((slices, detector), bf16),
            pltpu.VMEM((width, extended), bf16),
            pltpu.VMEM((slices, width), bf16),
            pltpu.VMEM((8, detector), f32),
            pltpu.VMEM((8, pixels + slices), f32),
            pltpu.VMEM((m, 8, pixels + slices), f32),
            chunk, chunk, chunk, chunk,
            pltpu.VMEM((chunks, slices, LANES), f32),
            edge, edge, edge, edge,
            dma, dma,
            dma((3,)), dma((3,)), dma((3,)), dma((3,)), dma((n,)), dma((n,)),
            dma((n,)), dma((n,)), dma((m,)), dma((m,)),
            *[dma((chunks * PARTS,))] * 4,
            dma((2,)), dma((2,)),
        ],
        compiler_params=pltpu.CompilerParams(
            collective_id=0, has_side_effects=True, vmem_limit_bytes=56 * 1024 * 1024
        ),
    )(volume, small, system[0], measured[0].reshape(2 * n, grain, detector))


def solution(mesh):
    return jax.shard_map(
        functools.partial(body, mesh.shape["slab"], mesh.shape["angle"]),
        mesh=mesh,
        in_specs=(
            P("slab", None),
            P("angle", None, None),
            P("angle", "slab", None),
            P(None, "angle", "slab"),
            P("angle", "slab"),
            P("angle", None),
            P("angle", None),
        ),
        out_specs=P("slab", None),
        check_vma=False,
    )
```

```python
import functools

import jax
import jax.numpy as jnp
from jax import lax
from jax.experimental import pallas as pl
from jax.experimental.pallas import tpu as pltpu
from jax.sharding import PartitionSpec as P

SMOOTHING = 0.5
TV_STEP = 0.2
FLOOR = 0.5
TILE = 512
FAR = 128
NEAR_ROWS = 144
FAR_ROWS = 80
PARTS = 2
LANES = 128


def smooth_slope(differ):
    return differ * lax.rsqrt(differ * differ + SMOOTHING * SMOOTHING)


def kernel(
    n, m, vol_ref, small_ref, sys_ref, meas_ref, out_ref,
    sysv, volx, smallx, win, fwd, inv, spread, band_t, band_own, col_sum, pack, packs,
    scale, acc, recv_a, recv_b, total, mid, edge_lo, edge_hi, halo_prev, halo_next,
    sys_sem, own_sem, vol_send, vol_recv, small_send, small_recv, win_send, win_recv,
    relay_send, relay_recv, pack_send, pack_recv, a_send, a_recv, b_send, b_recv, edge_send, edge_recv,
):
    me = lax.axis_index("slab")
    ang = lax.axis_index("angle")
    slices, pixels = vol_ref.shape
    detector = sysv.shape[1]
    width = 2 * slices
    chunks = pixels // LANES
    piece = slices // PARTS
    half = m // 2
    chip, core = me // 2, lax.rem(me, 2)
    partner = chip * 2 + 1 - core
    f32, bf16 = jnp.float32, jnp.bfloat16

    def slab_peer(k):
        return lax.rem(me + k, n)

    def angle_peer(k):
        return lax.rem(ang + k, m)

    def first_block(slab):
        return jnp.clip(2 * slab - 1, 0, 2 * n - 4)

    def remote(src, dst, send, recv, axis, peer):
        return pltpu.make_async_remote_copy(
            src_ref=src, dst_ref=dst, send_sem=send, recv_sem=recv,
            device_id={axis: peer}, device_id_type=pl.DeviceIdType.MESH,
        )

    extra = volx.shape[0] - slices
    volx[pl.ds(slices, extra), :] = jnp.zeros((extra, pixels), bf16)
    smallx[:, pl.ds(slices, extra)] = jnp.zeros((8, extra), f32)
    barrier = pltpu.get_barrier_semaphore()
    for k in range(1, n):
        pl.semaphore_signal(barrier, inc=1, device_id={"slab": slab_peer(k)},
                            device_id_type=pl.DeviceIdType.MESH)
    for k in range(1, m):
        pl.semaphore_signal(barrier, inc=1, device_id={"angle": angle_peer(k)},
                            device_id_type=pl.DeviceIdType.MESH)
    sys_copy = pltpu.make_async_copy(sys_ref, sysv, sys_sem)
    sys_copy.start()
    own_copy = pltpu.make_async_copy(meas_ref.at[pl.ds(first_block(me), 4)], win.at[me], own_sem)
    own_copy.start()
    own = pl.ds(0, slices)
    volx[own, :] = vol_ref[...].astype(bf16)
    smallx[:, own] = small_ref[...]
    has_prev, has_next = me > 0, me < n - 1
    prev_at, next_at, far_at = slices, 2 * slices, 3 * slices
    far_up = jnp.logical_or(me == 0, me == n - 3)
    far_down = jnp.logical_or(me == 2, me == n - 1)
    has_far = jnp.logical_or(far_up, far_down)

    pl.semaphore_wait(barrier, n + m - 2)

    def halo(slot, src_at, dst_at, size, src_row, dst_row, rows, peer):
        return (
            remote(smallx.at[:, pl.ds(src_at, size)], smallx.at[:, pl.ds(dst_at, size)],
                   small_send.at[slot], small_recv.at[slot], "slab", peer),
            remote(volx.at[pl.ds(src_row, rows)], volx.at[pl.ds(dst_row, rows)],
                   vol_send.at[slot], vol_recv.at[slot], "slab", peer),
        )

    above, under = lax.rem(me + 1, n), lax.rem(me + n - 1, n)
    cut = slices - NEAR_ROWS
    next_all = halo(0, 0, prev_at, slices, 0, prev_at, slices, above)
    next_part = halo(0, 0, prev_at, slices, cut, prev_at + cut, NEAR_ROWS, above)
    prev_all = halo(1, 0, next_at, slices, 0, next_at, slices, under)
    prev_part = halo(1, 0, next_at, slices, 0, next_at, NEAR_ROWS, under)
    far_cut = FAR - FAR_ROWS
    to_up = halo(2, slices - FAR, far_at, FAR, slices - FAR_ROWS, far_at + far_cut, FAR_ROWS,
                 lax.rem(me + 2, n))
    to_down = halo(2, 0, far_at, FAR, 0, far_at, FAR_ROWS, lax.rem(me + n - 2, n))
    both, either, no = jnp.logical_and, jnp.logical_or, jnp.logical_not
    send_up_all = either(me == 0, me == n - 2)
    send_down_all = either(me == n - 1, me == 1)
    get_prev_all = either(me == 1, me == n - 1)
    get_next_all = either(me == n - 2, me == 0)
    moves = (
        (both(has_next, send_up_all), next_all),
        (both(has_next, no(send_up_all)), next_part),
        (both(has_prev, send_down_all), prev_all),
        (both(has_prev, no(send_down_all)), prev_part),
        (far_up, to_up),
        (far_down, to_down),
    )
    arrivals = (
        (both(has_prev, get_prev_all), next_all),
        (both(has_prev, no(get_prev_all)), next_part),
        (both(has_next, get_next_all), prev_all),
        (both(has_next, no(get_next_all)), prev_part),
        (far_down, to_up),
        (far_up, to_down),
    )
    for condition, copies in moves:
        @pl.when(condition)
        def _():
            for copy in copies:
                copy.start()

    chips = n // 2
    shares, gets, relays, relay_gets = [], [], [], []
    shift = first_block(chip * 2 + 1) - first_block(chip * 2)
    relay_from = jnp.where(core == 0, shift, 3 - shift)
    for d in range(1, chips):
        for e in range(2):
            slot = 2 * d + e
            peer = lax.rem(chip + d, chips) * 2 + e
            shares.append(remote(
                meas_ref.at[pl.ds(first_block(peer) + e, 3)], win.at[me, pl.ds(e, 3)],
                win_send.at[slot], win_recv.at[2 * d + core], "slab", peer))
            source = lax.rem(chip + chips - d, chips) * 2 + e
            gets.append(remote(
                meas_ref.at[pl.ds(0, 3)], win.at[source, pl.ds(core, 3)],
                win_send.at[slot], win_recv.at[slot], "slab", peer))
            relays.append(remote(
                win.at[source, pl.ds(relay_from, 1)], win.at[source, pl.ds(3 * core, 1)],
                relay_send.at[slot], relay_recv.at[slot], "slab", partner))
            relay_gets.append(remote(
                win.at[source, pl.ds(relay_from, 1)], win.at[source, pl.ds(3 - 3 * core, 1)],
                relay_send.at[slot], relay_recv.at[slot], "slab", partner))
    beside = remote(meas_ref.at[pl.ds(first_block(partner), 4)], win.at[me],
                    win_send.at[0], win_recv.at[0], "slab", partner)
    beside_get = remote(meas_ref.at[pl.ds(0, 4)], win.at[partner],
                        win_send.at[0], win_recv.at[0], "slab", partner)
    for copy in shares + [beside]:
        copy.start()

    sys_copy.wait()
    col_sum[...] = jnp.dot(jnp.ones((8, pixels), bf16), sysv[...], preferred_element_type=f32)
    pixel_sum = lax.dot_general(jnp.ones((8, detector), bf16), sysv[...],
                                (((1,), (1,)), ((), ())), preferred_element_type=f32)
    keep = lax.broadcasted_iota(jnp.int32, (8, 1), 0) == 0
    pack[:, pl.ds(0, pixels)] = jnp.where(keep, pixel_sum, 0.0)
    weight_total = jnp.sum(small_ref[0:4, :], axis=0, keepdims=True)
    pack[:, pl.ds(pixels, slices)] = jnp.where(keep, weight_total, 0.0)
    packs[pl.ds(ang, 1)] = pack[...][None]
    pack_copies = [
        remote(pack, packs.at[ang], pack_send.at[k], pack_recv.at[k], "angle", angle_peer(k))
        for k in range(1, m)
    ]
    for copy in pack_copies:
        copy.start()

    for condition, copies in arrivals:
        @pl.when(condition)
        def _():
            for copy in copies:
                copy.wait_recv()

    share = width // n
    position = lax.broadcasted_iota(jnp.int32, (width, 1), 0)
    source = lax.shift_right_logical(position, share.bit_length() - 1)
    row = first_block(me) * (slices // 2) + lax.bitwise_and(position, share - 1) * n + source
    row = row.astype(f32)
    row_weight = jnp.zeros((width, 1), f32)
    for start in range(0, volx.shape[0], FAR):
        at = pl.ds(start, FAR)
        behind = row - smallx[4:5, at]
        block = jnp.zeros((width, FAR), f32)
        for k in range(4):
            block = jnp.where(behind == float(k), smallx[k : k + 1, at], block)
        row_weight = row_weight + jnp.sum(block, axis=1, keepdims=True)
        band_t[:, at] = block.astype(bf16)
        if start < slices:
            band_own[at, :] = block.T.astype(bf16)

    @pl.loop(0, detector // TILE)
    def _(step):
        at = pl.ds(pl.multiple_of(step * TILE, TILE), TILE)
        line = jnp.dot(volx[...], sysv[:, at], preferred_element_type=f32).astype(bf16)
        fwd[:, at] = jnp.dot(band_t[...], line, preferred_element_type=f32)
        inv[:, at] = 1.0 / jnp.maximum(row_weight * col_sum[0:1, at], FLOOR)

    for copy in pack_copies:
        copy.wait_recv()
    all_packs = packs[...].reshape(m * 8, pixels + slices)
    for part in range(PARTS):
        first = part * piece
        weight = lax.dot_general(
            all_packs[:, pixels + first : pixels + first + piece], all_packs[:, :pixels],
            (((0,), (0,)), ((), ())), precision=lax.Precision.HIGHEST, preferred_element_type=f32,
        )
        scale[pl.ds(first, piece), :] = 1.0 / weight

    own_copy.wait()
    for get, relay in zip(gets, relays):
        get.wait_recv()
        relay.start()
    beside_get.wait_recv()
    for get in relay_gets:
        get.wait_recv()

    @pl.loop(0, detector // TILE)
    def _(step):
        at = pl.ds(pl.multiple_of(step * TILE, TILE), TILE)
        rows = win[:, :, :, at].astype(f32).reshape(width, TILE)
        residual = ((rows - fwd[:, at]) * inv[:, at]).astype(bf16)
        spread[:, at] = jnp.dot(band_own[...], residual, preferred_element_type=f32).astype(bf16)

    left = ang < half
    inner = jnp.where(left, ang + 1, ang - 1)
    outer = jnp.where(left, jnp.maximum(ang - 1, 0), jnp.minimum(ang + 1, m - 1))
    centre = jnp.logical_or(ang == half - 1, ang == half)
    has_outer = jnp.logical_and(ang > 0, ang < m - 1)
    not_centre = jnp.logical_not(centre)
    no_outer = jnp.logical_not(has_outer)

    def up_copy(c, target):
        sem = a_recv if target is recv_a else b_recv
        return remote(acc.at[c], target.at[c], a_send.at[c], sem.at[c], "angle", inner)

    def down_copy(c):
        return remote(total.at[c], recv_b.at[c], b_send.at[c], b_recv.at[c], "angle", outer)

    def multiply(pair):
        product = lax.dot_general(spread[...], sysv[pl.ds(pair * 2 * LANES, 2 * LANES), :],
                                  (((1,), (1,)), ((), ())), preferred_element_type=f32)
        for c in range(2):
            for part in range(PARTS):
                acc[(2 * pair + c) * PARTS + part] = product[
                    part * piece : (part + 1) * piece, c * LANES : (c + 1) * LANES
                ]

    def collect(c):
        @pl.when(has_outer)
        def _():
            up_copy(c, recv_a).wait_recv()
            acc[c] = acc[c] + recv_a[c]

        @pl.when(centre)
        def _():
            up_copy(c, recv_b).start()

        @pl.when(not_centre)
        def _():
            up_copy(c, recv_a).start()

    def finish(index):
        down_copy(index).wait_recv()
        c, part = index // PARTS, index % PARTS
        first = part * piece
        whole = jnp.where(centre, acc[index] + recv_b[index], recv_b[index])
        total[index] = whole

        @pl.when(has_outer)
        def _():
            down_copy(index).start()

        rows = pl.ds(first, piece)
        at = pl.ds(c * LANES, LANES)
        cells = vol_ref[rows, at] + whole * scale[rows, at]
        mid[c, rows] = cells
        if part == 0:
            edge_lo[c : c + 1, :] = cells[0:1, :]
        if part == PARTS - 1:
            edge_hi[c : c + 1, :] = cells[piece - 1 : piece, :]

    pieces = chunks * PARTS

    def run(lag):
        for index in range(pieces + lag):
            if index < pieces:
                if index % (2 * PARTS) == 0:
                    multiply(index // (2 * PARTS))
                collect(index)
            if index >= lag:
                finish(index - lag)

    @pl.when(has_outer)
    def _():
        run(2)

    @pl.when(no_outer)
    def _():
        run(pieces)

    edge_up = remote(edge_hi, halo_prev, edge_send.at[0], edge_recv.at[0], "slab", lax.rem(me + 1, n))
    edge_down = remote(edge_lo, halo_next, edge_send.at[1], edge_recv.at[1], "slab", lax.rem(me + n - 1, n))

    @pl.when(has_next)
    def _():
        edge_up.start()

    @pl.when(has_prev)
    def _():
        edge_down.start()

    @pl.when(jnp.logical_not(has_prev))
    def _():
        halo_prev[...] = edge_lo[...]

    @pl.when(jnp.logical_not(has_next))
    def _():
        halo_next[...] = edge_hi[...]

    lane = lax.broadcasted_iota(jnp.int32, (1, LANES), 1)
    below = None
    for c in range(chunks):
        cells = mid[c]
        slope = jnp.where(lane < LANES - 1,
                          smooth_slope(pltpu.roll(cells, LANES - 1, axis=1) - cells), 0.0)
        gradient = pltpu.roll(slope, 1, axis=1) - slope
        if below is not None:
            gradient = gradient + below
        if c + 1 < chunks:
            below = smooth_slope(mid[c + 1] - cells)
            gradient = gradient - below
        total_at = pl.ds(c * LANES, LANES)
        out_ref[:, total_at] = gradient

    @pl.when(has_prev)
    def _():
        edge_up.wait_recv()

    @pl.when(has_next)
    def _():
        edge_down.wait_recv()

    for c in range(chunks):
        at = pl.ds(c * LANES, LANES)
        cells = mid[c]
        upper = jnp.concatenate([cells[1:, :], halo_next[c : c + 1, :]], axis=0)
        slope = smooth_slope(upper - cells)
        first = smooth_slope(cells[0:1, :] - halo_prev[c : c + 1, :])
        lower = jnp.concatenate([first, slope[: slices - 1, :]], axis=0)
        out_ref[:, at] = cells - TV_STEP * (out_ref[:, at] + lower - slope)

    for condition, copies in moves:
        @pl.when(condition)
        def _():
            for copy in copies:
                copy.wait_send()
    for copy in shares + [beside] + relays + pack_copies:
        copy.wait_send()
    for c in range(pieces):
        up_copy(c, recv_a).wait_send()

        @pl.when(has_outer)
        def _():
            down_copy(c).wait_send()

    @pl.when(has_next)
    def _():
        edge_up.wait_send()

    @pl.when(has_prev)
    def _():
        edge_down.wait_send()


def body(n, m, volume, system, measured, band_weight, band_offset, row_first, row_count):
    slices, pixels = volume.shape
    detector = system.shape[2]
    grain = slices // 2 // n
    width = 2 * slices
    chunks = pixels // LANES
    extended = 3 * slices + FAR
    small = jnp.concatenate(
        [
            band_weight[:, 0, :].astype(jnp.float32),
            band_offset.astype(jnp.float32),
            jnp.zeros((3, slices), jnp.float32),
        ],
        axis=0,
    )
    f32, bf16 = jnp.float32, jnp.bfloat16
    dma = pltpu.SemaphoreType.DMA
    chunk = pltpu.VMEM((chunks * PARTS, slices // PARTS, LANES), f32)
    edge = pltpu.VMEM((chunks, LANES), f32)
    vmem = pl.BlockSpec(memory_space=pltpu.VMEM)
    return pl.pallas_call(
        functools.partial(kernel, n, m),
        out_shape=jax.ShapeDtypeStruct((slices, pixels), f32),
        in_specs=[vmem, vmem, pl.BlockSpec(memory_space=pl.ANY), pl.BlockSpec(memory_space=pl.ANY)],
        out_specs=vmem,
        scratch_shapes=[
            pltpu.VMEM((pixels, detector), bf16),
            pltpu.VMEM((extended, pixels), bf16),
            pltpu.VMEM((8, extended), f32),
            pltpu.VMEM((n, 4, grain, detector), bf16),
            pltpu.VMEM((width, detector), f32),
            pltpu.VMEM((width, detector), f32),
            pltpu.VMEM((slices, detector), bf16),
            pltpu.VMEM((width, extended), bf16),
            pltpu.VMEM((slices, width), bf16),
            pltpu.VMEM((8, detector), f32),
            pltpu.VMEM((8, pixels + slices), f32),
            pltpu.VMEM((m, 8, pixels + slices), f32),
            pltpu.VMEM((slices, pixels), f32),
            chunk, chunk, chunk, chunk,
            pltpu.VMEM((chunks, slices, LANES), f32),
            edge, edge, edge, edge,
            dma, dma,
            dma((3,)), dma((3,)), dma((3,)), dma((3,)), dma((n,)), dma((n,)),
            dma((n,)), dma((n,)), dma((m,)), dma((m,)),
            *[dma((chunks * PARTS,))] * 4,
            dma((2,)), dma((2,)),
        ],
        compiler_params=pltpu.CompilerParams(
            collective_id=0, has_side_effects=True, vmem_limit_bytes=56 * 1024 * 1024
        ),
    )(volume, small, system[0], measured[0].reshape(2 * n, grain, detector))


def solution(mesh):
    return jax.shard_map(
        functools.partial(body, mesh.shape["slab"], mesh.shape["angle"]),
        mesh=mesh,
        in_specs=(
            P("slab", None),
            P("angle", None, None),
            P("angle", "slab", None),
            P(None, "angle", "slab"),
            P("angle", "slab"),
            P("angle", None),
            P("angle", None),
        ),
        out_specs=P("slab", None),
        check_vma=False,
    )
```
